32 devices in a mesh: ctx: 16 (over z, y, core), fsdp: 2 (over x).
Axes of the slice: x: 2, y: 2, z: 4, core: 2. Of those that a mesh axis runs over, the one named last changes fastest.
Arguments:
- queries: bfloat16 [2, 2048, 2048], P('fsdp', 'ctx'), may hold values from -8 to 8
- keys_values: bfloat16 [2, 2048, 2, 2048], P('fsdp', 'ctx'), may hold values from -8 to 8
- upstream: bfloat16 [2, 2048, 2048], P('fsdp', 'ctx'), may hold values from -6 to 6
- out_weight: bfloat16 [2048, 2048], P('fsdp'), may hold values from -0.125 to 0.125
Outputs:
- grad_queries: bfloat16 [2, 2048, 2048], P('fsdp', 'ctx')
- grad_keys_values: bfloat16 [2, 2048, 2, 2048], P('fsdp', 'ctx')
- grad_weight: float32 [2048, 2048], P(('ctx', 'fsdp'))
The draws below stay inside these ranges and needn't reach their ends.
All inputs are finite; a program needn't handle non-finite values.
Results may differ from the reference program's by a relative error of at most 0.014.
Values may be sent and summed in bfloat16 or wider, within the bound.
A program may use at most 128 MiB of HBM per device.

```python
import jax
import jax.numpy as jnp
from jax import lax

D = 2048
HEADS = 16
HEAD_DIM = 128
ATTN = 2048
TOK_DEV = 128
SPAN = 4
WINDOW = 512
SEQ_DEV = 1
SEQ = 2048
SEQS = 2
N_CTX = 16
N_FSDP = 2


def draw_queries(key, part):
    result = jnp.clip(jax.random.normal(jax.random.fold_in(key, 11), (SEQS, SEQ, ATTN), jnp.float32), -4.0, 4.0)
    return result.astype(jnp.bfloat16)


def draw_keys_values(key, part):
    key_part = jnp.clip(jax.random.normal(jax.random.fold_in(key, 21), (SEQS, SEQ, ATTN), jnp.float32), -4.0, 4.0)
    value_part = jnp.clip(jax.random.normal(jax.random.fold_in(key, 23), (SEQS, SEQ, ATTN), jnp.float32), -4.0, 4.0)
    return jnp.stack([key_part, value_part], axis=2).astype(jnp.bfloat16)


def spiked(values, own_key, source, target, parts, factor):
    def block_of(axis_at):
        return (jnp.arange(values.shape[axis_at]) // (values.shape[axis_at] // parts)).reshape((-1,) + (1,) * (values.ndim - 1 - axis_at))

    near = jax.random.permutation(own_key, parts)[block_of(target)]
    other_side = (block_of(target) + parts // 2) % parts
    return jnp.where((block_of(source) == near) | (block_of(source) == other_side), factor * values, values)


def levels(stream_key, dims, cuts, smallest, top_value):
    level, own = 1.0, jax.random.fold_in(stream_key, 6)
    for axis_at, parts in cuts:
        steps = jnp.exp(jax.random.uniform(jax.random.fold_in(own, axis_at), (parts,), jnp.float32, smallest / len(cuts), top_value / len(cuts)))
        level = level * jnp.repeat(steps, dims[axis_at] // parts).reshape([-1 if axis == axis_at else 1 for axis in range(len(dims))])
    return level


def scatter_about(rng, shape, width, reach, split=(), kind=jnp.bfloat16):
    drawn = jax.random.normal(rng, shape, jnp.float32) * width
    if len(split) > 0:
        drawn = levels(rng, shape, split, -0.22, 0.18) * drawn
    return jnp.clip(drawn, min=-reach, max=reach).astype(kind)


def gaussian_with(own_key, dims, width, bound, cuts, heavy, kind=jnp.bfloat16):
    values = width * jax.random.normal(own_key, dims, jnp.float32)
    if cuts:
        values = values * levels(own_key, dims, cuts, -0.22, 0.18)
    return jnp.clip(spiked(values, jax.random.fold_in(own_key, 3), *heavy), -bound, bound).astype(kind)


def setup_inputs(seed: int = 0) -> dict:
    key_of = jax.random.split(jax.random.key(seed), 5)
    queries = draw_queries(jax.random.fold_in(key_of[4], 71), 0)
    keys_values = draw_keys_values(jax.random.fold_in(key_of[4], 71), 0)
    upstream = gaussian_with(key_of[2], (SEQS, SEQ, D), 1.0, 6.0, ((0, 2), (1, 16)), (1, 2, 16, 2.0))
    out_weight = scatter_about(key_of[3], (D, ATTN), ATTN ** -0.5, 0.125, ((0, 2),))
    return {"queries": queries, "keys_values": keys_values, "upstream": upstream, "out_weight": out_weight}


NEGATIVE = -1e30


def one_sequence(inputs):
    query_seq, pair_seq, grad_seq = inputs
    padding = SPAN * TOK_DEV
    key_count = (SPAN + 1) * TOK_DEV
    inv_root = HEAD_DIM ** -0.5
    padded_pairs = jnp.concatenate([jnp.zeros((padding, 2, ATTN), jnp.bfloat16), pair_seq], axis=0)

    def block_step(carried, block_index):
        first_row = (block_index * TOK_DEV).astype(jnp.int32)
        query_block = lax.dynamic_slice_in_dim(query_seq, first_row, TOK_DEV, 0).astype(jnp.float32).reshape(TOK_DEV, HEADS, HEAD_DIM)
        grad_block = lax.dynamic_slice_in_dim(grad_seq, first_row, TOK_DEV, 0).reshape(TOK_DEV, HEADS, HEAD_DIM)
        pair_window = lax.dynamic_slice_in_dim(padded_pairs, first_row, key_count, 0)
        key_heads = pair_window[:, 0].astype(jnp.float32).reshape(key_count, HEADS, HEAD_DIM)
        value_heads = pair_window[:, 1].astype(jnp.float32).reshape(key_count, HEADS, HEAD_DIM)
        query_pos = first_row + jnp.arange(TOK_DEV, dtype=jnp.int32)
        key_pos = first_row - padding + jnp.arange(key_count, dtype=jnp.int32)
        distance = query_pos[:, None] - key_pos[None, :]
        visible = (distance >= 0) & (distance < WINDOW) & (key_pos[None, :] >= 0)
        scores = jnp.einsum('qhe,khe->hqk', query_block, key_heads) * inv_root
        scores = jnp.where(visible[None], scores, NEGATIVE)
        row_max = jnp.max(scores, axis=-1, keepdims=True)
        lifted = jnp.exp(scores - row_max)
        probability = lifted / jnp.sum(lifted, axis=-1, keepdims=True)
        probs_low = probability.astype(jnp.bfloat16)
        attended = jnp.einsum('hqk,khe->qhe', probs_low.astype(jnp.float32), value_heads).astype(jnp.bfloat16)
        grad_f = grad_block.astype(jnp.float32)
        products = jnp.einsum('qhe,khe->hqk', grad_f, value_heads)
        center = jnp.sum(grad_f * attended.astype(jnp.float32), axis=-1)
        center = jnp.swapaxes(center, 0, 1)[:, :, None]
        grad_scores = (probability * (products - center)).astype(jnp.bfloat16).astype(jnp.float32)
        grad_queries = (jnp.einsum('hqk,khe->qhe', grad_scores, key_heads) * inv_root).astype(jnp.bfloat16)
        grad_keys = jnp.einsum('hqk,qhe->khe', grad_scores, query_block) * inv_root
        grad_values = jnp.einsum('hqk,qhe->khe', probs_low.astype(jnp.float32), grad_f)
        grad_window = jnp.stack([grad_keys.reshape(key_count, ATTN), grad_values.reshape(key_count, ATTN)], axis=1)
        previous = lax.dynamic_slice_in_dim(carried, first_row, key_count, 0)
        carried = lax.dynamic_update_slice_in_dim(carried, previous + grad_window, first_row, 0)
        return carried, (attended.reshape(TOK_DEV, ATTN), grad_queries.reshape(TOK_DEV, ATTN))

    start_carry = jnp.zeros((SEQ + padding, 2, ATTN), jnp.float32)
    carried, outputs = lax.scan(block_step, start_carry, jnp.arange(N_CTX, dtype=jnp.int32))
    attended_all = outputs[0].reshape(SEQ, ATTN)
    grad_query_all = outputs[1].reshape(SEQ, ATTN)
    return attended_all, grad_query_all, carried[padding:].astype(jnp.bfloat16)


def reference(queries, keys_values, upstream, out_weight):
    grad_attended = jnp.dot(upstream.reshape(SEQS * SEQ, D), out_weight, preferred_element_type=jnp.float32)
    grad_attended = grad_attended.astype(jnp.bfloat16).reshape(SEQS, SEQ, ATTN)
    attended, grad_queries, grad_keys_values = lax.map(one_sequence, (queries, keys_values, grad_attended))
    attended_dev = attended.reshape(N_FSDP, SEQ_DEV, N_CTX, TOK_DEV, ATTN).transpose(0, 2, 1, 3, 4)
    attended_dev = attended_dev.reshape(N_FSDP * N_CTX, SEQ_DEV * TOK_DEV, ATTN)
    upstream_dev = upstream.reshape(N_FSDP, SEQ_DEV, N_CTX, TOK_DEV, D).transpose(0, 2, 1, 3, 4)
    upstream_dev = upstream_dev.reshape(N_FSDP * N_CTX, SEQ_DEV * TOK_DEV, D)

    def add_partial(running, pieces):
        weight_term = lax.dot_general(pieces[0], pieces[1], (((0,), (0,)), ((), ())), preferred_element_type=jnp.float32)
        weight_term = lax.optimization_barrier(weight_term.astype(jnp.bfloat16)).astype(jnp.float32)
        return running + weight_term, None

    grad_weight, unused_out = lax.scan(add_partial, jnp.zeros((D, ATTN), jnp.float32), (upstream_dev, attended_dev))
    return grad_queries, grad_keys_values, grad_weight
```

```python
import functools

import jax
import jax.numpy as jnp
from jax import lax
from jax.experimental import pallas as pl
from jax.experimental.pallas import tpu as pltpu
from jax.sharding import PartitionSpec as P

HEADS = 16
HEAD_DIM = 128
SPAN = 4
WINDOW = 512
NEGATIVE = -1e30
CHUNKS = 8
F32 = jnp.float32
BF16 = jnp.bfloat16


class Place:
    def __init__(self, planes, fsdp):
        self.planes, self.fsdp = planes, fsdp
        me = lax.axis_index("ctx")
        self.f = lax.axis_index("fsdp")
        self.p = lax.div(me, SPAN)
        self.r = lax.rem(me, SPAN)
        self.core = lax.rem(self.r, 2)
        self.y = lax.div(self.r, 2)
        self.mate = self.r + 1 - 2 * self.core
        self.across = lax.rem(self.r + 2, SPAN)

    def dev(self, p, r, f):
        return {"ctx": p * SPAN + r, "fsdp": f}

    def members(self):
        for dr in range(SPAN):
            for df in range(self.fsdp):
                if dr or df:
                    yield lax.rem(self.r + dr, SPAN), lax.rem(self.f + df, self.fsdp), dr, df

    def barrier(self):
        sem = pltpu.get_barrier_semaphore()
        count = 0
        for r, f, _, _ in self.members():
            pl.semaphore_signal(sem, inc=1, device_id=self.dev(self.p, r, f), device_id_type=pl.DeviceIdType.MESH)
            count += 1
        for dp in range(1, self.planes):
            other = lax.rem(self.p + dp, self.planes)
            pl.semaphore_signal(sem, inc=1, device_id=self.dev(other, self.r, self.f), device_id_type=pl.DeviceIdType.MESH)
            count += 1
        pl.semaphore_wait(sem, count)


def remote(src, dst, send, recv, device):
    return pltpu.make_async_remote_copy(
        src_ref=src, dst_ref=dst, send_sem=send, recv_sem=recv, device_id=device, device_id_type=pl.DeviceIdType.MESH
    )


def chunk_of(ref, c, rows):
    per = CHUNKS // 2
    return ref.at[lax.div(c, per), pl.ds(pl.multiple_of(lax.rem(c, per) * rows, rows), rows)]


def gather_kernel(
    planes, fsdp,
    kv, up, up_cols, weight,
    win, grad_att, up_all,
    w_v, up_in, part_out, part_in, zeros,
    z_send, y_send, c_send, s_send, slot_recv, zero_sem, w_sem, u_send, u_recv, q_send, q_recv, m_send, m_recv, own_sem,
):
    at = Place(planes, fsdp)
    toks = up.shape[0]
    depth = weight.shape[0]
    width = weight.shape[1]
    rows = 2 * toks // CHUNKS
    f = at.f
    mine = at.r * fsdp + f
    w_copy = pltpu.make_async_copy(weight, w_v, w_sem)
    w_copy.start()
    zeros[...] = jnp.zeros_like(zeros)
    own_cols = pltpu.make_async_copy(up_cols.at[mine], up_all.at[mine], own_sem)
    own_cols.start()
    at.barrier()

    def up_copy(df):
        g = lax.rem(f + df, fsdp)
        return remote(
            up.at[:, pl.ds(pl.multiple_of(g * depth, 128), depth)], up_in.at[fsdp - df], u_send.at[df], u_recv.at[fsdp - df],
            at.dev(at.p, at.r, g),
        )

    def slot(j, c):
        return chunk_of(win.at[j], c, rows)

    def z_copy(c):
        return remote(chunk_of(kv, c, rows), slot(at.r, c), z_send.at[c], slot_recv.at[at.r, c], at.dev(at.p + 1, at.r, f))

    def y_copy(c, src):
        return remote(src, slot(at.r, c), y_send.at[c], slot_recv.at[at.r, c], at.dev(at.p, at.across, f))

    def c_copy(c, src):
        return remote(src, slot(at.r, c), c_send.at[c], slot_recv.at[at.r, c], at.dev(at.p, at.mate, f))

    def s_copy(c):
        return remote(slot(at.across, c), slot(at.across, c), s_send.at[c], slot_recv.at[at.across, c], at.dev(at.p, at.mate, f))

    def arrived(j, c):
        remote(slot(j, c), slot(j, c), z_send.at[c], slot_recv.at[j, c], at.dev(at.p, at.mate, f)).wait_recv()

    def zero_copy(c):
        return pltpu.make_async_copy(zeros, slot(at.r, c), zero_sem.at[c])

    for df in range(1, fsdp):
        up_copy(df).start()

    def begin(c, _):
        @pl.when(at.p < planes - 1)
        def _():
            z_copy(c).start()

        @pl.when(at.p == 0)
        def _():
            zero_copy(c).start()

        @pl.when(at.y == 0)
        def _():
            y_copy(c, chunk_of(kv, c, rows)).start()

        @pl.when(at.core == 0)
        def _():
            c_copy(c, chunk_of(kv, c, rows)).start()

        return 0

    lax.fori_loop(0, CHUNKS, begin, 0)

    def col_copy(r, g, dr, df):
        there = r * fsdp + g
        return remote(up_cols.at[there], up_all.at[mine], m_send.at[dr, df], m_recv.at[dr, df], at.dev(at.p, r, g))

    for r, g, dr, df in at.members():
        col_copy(r, g, dr, df).start()
    w_copy.wait()
    tile = 512

    def product(lhs_of, put):
        def step(t, _):
            cols = pl.ds(pl.multiple_of(t * tile, tile), tile)
            put(cols, jnp.dot(lhs_of(), w_v[:, cols], preferred_element_type=F32))
            return 0

        lax.fori_loop(0, width // tile, step, 0)

    def part_copy(df):
        return remote(
            part_out.at[df], part_in.at[fsdp - df], q_send.at[df], q_recv.at[fsdp - df],
            at.dev(at.p, at.r, lax.rem(f + df, fsdp)),
        )

    for df in range(1, fsdp):
        remote(up_in.at[df], up_in.at[df], u_send.at[df], u_recv.at[df], at.dev(at.p, at.r, lax.rem(f + df, fsdp))).wait_recv()

        def put(cols, value, df=df):
            part_out[df, :, cols] = value.astype(BF16)

        product(lambda df=df: up_in[df], put)
        part_copy(df).start()

    def forward(c, _):
        @pl.when(at.p == 0)
        def _():
            zero_copy(c).wait()

        @pl.when(at.p > 0)
        def _():
            arrived(at.r, c)

        @pl.when(at.y == 1)
        def _():
            y_copy(c, slot(at.r, c)).start()

        @pl.when(at.core == 1)
        def _():
            c_copy(c, slot(at.r, c)).start()

        return 0

    def share(c, _):
        arrived(at.across, c)
        s_copy(c).start()
        return 0

    def both(c, _):
        forward(c, 0)
        share(c, 0)
        return 0

    lax.fori_loop(0, CHUNKS, both, 0)
    own_depth = pl.ds(pl.multiple_of(f * depth, 128), depth)
    for df in range(1, fsdp):
        remote(part_in.at[df], part_in.at[df], q_send.at[df], q_recv.at[df], at.dev(at.p, at.r, lax.rem(f + df, fsdp))).wait_recv()

    def put_own(cols, value):
        for df in range(1, fsdp):
            value = value + part_in[df, :, cols].astype(F32)
        grad_att[:, cols] = value.astype(BF16)

    product(lambda: up[:, own_depth], put_own)

    def finish(c, _):
        arrived(at.mate, c)
        arrived(lax.rem(at.mate + 2, SPAN), c)

        @pl.when(at.p < planes - 1)
        def _():
            z_copy(c).wait_send()

        y_copy(c, slot(at.r, c)).wait_send()
        c_copy(c, slot(at.r, c)).wait_send()
        s_copy(c).wait_send()
        return 0

    lax.fori_loop(0, CHUNKS, finish, 0)
    for df in range(1, fsdp):
        up_copy(df).wait_send()
        part_copy(df).wait_send()
    own_cols.wait()
    for r, g, dr, df in at.members():
        col_copy(r, g, dr, df).wait_send()
        back = lax.rem(at.r + SPAN - dr, SPAN) * fsdp + lax.rem(f + fsdp - df, fsdp)
        remote(up_all.at[back], up_all.at[back], m_send.at[dr, df], m_recv.at[dr, df], at.dev(at.p, r, g)).wait_recv()


def attend_kernel(q_ref, kv_ref, win_ref, ga_ref, dq_ref, att_ref, dkv_ref, dwin_ref):
    me = lax.axis_index("ctx")
    toks = q_ref.shape[0]
    inv_root = HEAD_DIM ** (-0.5)
    r = lax.rem(me, SPAN)
    first_plane = lax.div(me, SPAN) == 0
    row = lax.broadcasted_iota(jnp.int32, (toks, toks), 0)
    col = lax.broadcasted_iota(jnp.int32, (toks, toks), 1)
    masks = []
    for j in range(SPAN):
        blocks = jnp.where(j < r, r - j, r - j + SPAN)
        distance = blocks * toks + row - col
        limit = jnp.where(jnp.logical_and(first_plane, j >= r), 0, WINDOW)
        masks.append((distance >= 0) & (distance < limit))
    masks.append((row - col >= 0) & (row - col < WINDOW))
    mask = jnp.concatenate(masks, axis=1)
    nt = (((1,), (1,)), ((), ()))
    tn = (((0,), (0,)), ((), ()))
    for h in range(q_ref.shape[1] // HEAD_DIM):
        cols = slice(h * HEAD_DIM, (h + 1) * HEAD_DIM)
        q = q_ref[:, cols]
        ga = ga_ref[:, cols]
        k = jnp.concatenate([win_ref[j, 0, :, cols] for j in range(SPAN)] + [kv_ref[0, :, cols]], axis=0)
        v = jnp.concatenate([win_ref[j, 1, :, cols] for j in range(SPAN)] + [kv_ref[1, :, cols]], axis=0)
        scores = lax.dot_general(q, k, nt, preferred_element_type=F32) * inv_root
        scores = jnp.where(mask, scores, NEGATIVE)
        lifted = jnp.exp(scores - jnp.max(scores, axis=-1, keepdims=True))
        prob = lifted * (1.0 / jnp.sum(lifted, axis=-1, keepdims=True))
        low = prob.astype(BF16)
        att = jnp.dot(low, v, preferred_element_type=F32).astype(BF16)
        att_ref[:, cols] = att
        products = lax.dot_general(ga, v, nt, preferred_element_type=F32)
        center = jnp.sum(ga.astype(F32) * att.astype(F32), axis=-1, keepdims=True)
        ds = (prob * (products - center)).astype(BF16)
        dq_ref[:, cols] = (jnp.dot(ds, k, preferred_element_type=F32) * inv_root).astype(BF16)
        dk = lax.dot_general(ds, q, tn, preferred_element_type=F32) * inv_root
        dv = lax.dot_general(low, ga, tn, preferred_element_type=F32)
        for j in range(SPAN):
            dwin_ref[j, 0, :, cols] = dk[j * toks : (j + 1) * toks].astype(BF16)
            dwin_ref[j, 1, :, cols] = dv[j * toks : (j + 1) * toks].astype(BF16)
        dkv_ref[0, :, cols] = dk[SPAN * toks :]
        dkv_ref[1, :, cols] = dv[SPAN * toks :]


def return_kernel(
    planes, fsdp,
    dwin, dkv, att, up_all,
    out_kv, out_w,
    g, share_in, y_in, c_in, z_in, att_all, w_out, w_in,
    load_sem, sh_send, sh_recv, y_send, y_recv, c_send, c_recv, z_send, z_recv,
    a_send, a_recv, b_send, b_recv, o_sem, w_send, w_recv,
):
    at = Place(planes, fsdp)
    toks = att.shape[0]
    rows = 2 * toks // CHUNKS
    width = att.shape[1]
    f = at.f
    mine = at.r * fsdp + f
    mates = at.mate * fsdp + f
    loads = [pltpu.make_async_copy(dwin.at[j], g.at[j], load_sem.at[j]) for j in range(SPAN)]
    for load in loads:
        load.start()
    own = pltpu.make_async_copy(att, att_all.at[mine], o_sem)
    own.start()
    at.barrier()

    def peers():
        for half in range(2):
            for df in range(fsdp):
                yield half, df, lax.rem(at.r + 2 * half, SPAN), lax.rem(f + df, fsdp)

    def a_copy(half, df, r, h):
        return remote(att, att_all.at[mine], a_send.at[half, df], a_recv.at[half, df], at.dev(at.p, r, h))

    def origin(half, df):
        return lax.rem(at.r + SPAN - 2 * half, SPAN) * fsdp + lax.rem(f + fsdp - df, fsdp)

    def b_copy(half, df):
        block = origin(half, df)
        src = att if half == 0 and df == 0 else att_all.at[block]
        return remote(src, att_all.at[block], b_send.at[half, df], b_recv.at[half, df], at.dev(at.p, at.mate, f))

    for half, df, r, h in peers():
        if half or df:
            a_copy(half, df, r, h).start()
    b_copy(0, 0).start()
    for load in loads:
        load.wait()

    def part(ref, c):
        return chunk_of(ref, c, rows)

    mate_across = lax.rem(at.mate + 2, SPAN)

    def sh_copy(c):
        return remote(part(g.at[mate_across], c), part(share_in, c), sh_send.at[c], sh_recv.at[c], at.dev(at.p, at.mate, f))

    def c_copy(c):
        return remote(part(g.at[at.mate], c), part(c_in, c), c_send.at[c], c_recv.at[c], at.dev(at.p, at.mate, f))

    def y_copy(c):
        return remote(part(g.at[at.across], c), part(y_in, c), y_send.at[c], y_recv.at[c], at.dev(at.p, at.across, f))

    def z_copy(c):
        return remote(part(g.at[at.r], c), part(z_in, c), z_send.at[c], z_recv.at[c], at.dev(at.p - 1, at.r, f))

    def first(c, _):
        sh_copy(c).start()
        c_copy(c).start()
        return 0

    lax.fori_loop(0, CHUNKS, first, 0)

    def where(c):
        per = CHUNKS // 2
        return lax.div(c, per), pl.ds(pl.multiple_of(lax.rem(c, per) * rows, rows), rows)

    def second(c, _):
        kv, span = where(c)
        sh_copy(c).wait_recv()
        g[at.across, kv, span] = (g[at.across, kv, span].astype(F32) + share_in[kv, span].astype(F32)).astype(BF16)
        y_copy(c).start()
        return 0

    lax.fori_loop(0, CHUNKS, second, 0)

    own.wait()
    for half, df, r, h in peers():
        if half or df:
            block = origin(half, df)
            remote(att_all.at[block], att_all.at[block], a_send.at[half, df], a_recv.at[half, df], at.dev(at.p, r, h)).wait_recv()
            b_copy(half, df).start()

    def third(c, _):
        kv, span = where(c)
        c_copy(c).wait_recv()
        y_copy(c).wait_recv()
        core_prev = at.core == 1
        y_prev = at.y == 1
        c_val = c_in[kv, span].astype(F32)
        y_val = y_in[kv, span].astype(F32)
        zero = jnp.zeros_like(c_val)
        prev = g[at.r, kv, span].astype(F32) + jnp.where(core_prev, c_val, zero) + jnp.where(y_prev, y_val, zero)
        g[at.r, kv, span] = prev.astype(BF16)
        dkv[kv, span] = dkv[kv, span] + jnp.where(core_prev, zero, c_val) + jnp.where(y_prev, zero, y_val)

        @pl.when(at.p > 0)
        def _():
            z_copy(c).start()

        return 0

    lax.fori_loop(0, CHUNKS, third, 0)

    for half, df, r, h in peers():
        block = lax.rem(at.mate + SPAN - 2 * half, SPAN) * fsdp + lax.rem(f + fsdp - df, fsdp)
        remote(att_all.at[block], att_all.at[block], b_send.at[half, df], b_recv.at[half, df], at.dev(at.p, at.mate, f)).wait_recv()
    tile = 256
    own_rows = out_w.shape[0]
    tn = (((0,), (0,)), ((), ()))
    tokens = SPAN * fsdp * toks
    lhs = up_all[...].reshape(tokens, up_all.shape[2])

    def mul(t, _):
        cols = pl.ds(pl.multiple_of(t * tile, tile), tile)
        value = lax.dot_general(lhs, att_all[:, :, cols].reshape(tokens, tile), tn, preferred_element_type=F32)
        out_w[:, cols] = jnp.zeros((own_rows, tile), F32)
        for q in range(planes):
            w_out[q, :, cols] = value[q * own_rows : (q + 1) * own_rows].astype(BF16)
        return 0

    lax.fori_loop(0, width // tile, mul, 0)

    def w_copy(dp):
        other = lax.rem(at.p + dp, planes)
        return remote(w_out.at[other], w_in.at[planes - dp], w_send.at[dp], w_recv.at[planes - dp], at.dev(other, at.r, f))

    for dp in range(1, planes):
        w_copy(dp).start()

    def fourth(c, _):
        kv, span = where(c)

        @pl.when(at.p < planes - 1)
        def _():
            z_copy(c).wait_recv()
            out_kv[kv, span] = (dkv[kv, span] + z_in[kv, span].astype(F32)).astype(BF16)

        @pl.when(at.p == planes - 1)
        def _():
            out_kv[kv, span] = dkv[kv, span].astype(BF16)

        sh_copy(c).wait_send()
        c_copy(c).wait_send()
        y_copy(c).wait_send()

        @pl.when(at.p > 0)
        def _():
            z_copy(c).wait_send()

        return 0

    lax.fori_loop(0, CHUNKS, fourth, 0)
    out_w[...] = w_out[at.p].astype(F32)
    for dp in range(1, planes):
        remote(w_in.at[dp], w_in.at[dp], w_send.at[dp], w_recv.at[dp], at.dev(lax.rem(at.p + dp, planes), at.r, f)).wait_recv()
        out_w[...] += w_in[dp].astype(F32)
    for dp in range(1, planes):
        w_copy(dp).wait_send()
    for half, df, r, h in peers():
        if half or df:
            a_copy(half, df, r, h).wait_send()
        b_copy(half, df).wait_send()


def shards(queries, keys_values, upstream, out_weight):
    seqs, toks, width = queries.shape
    ctx, fsdp = lax.axis_size("ctx"), lax.axis_size("fsdp")
    planes = ctx // SPAN
    model = upstream.shape[2]
    own_rows = model // (ctx * fsdp)
    group = SPAN * fsdp
    cols = planes * own_rows
    depth = out_weight.shape[0]
    kv = jnp.swapaxes(keys_values[0], 0, 1)
    up = upstream[0]
    up_cols = up.reshape(toks, planes, SPAN, fsdp, own_rows).transpose(2, 3, 0, 1, 4).reshape(group, toks, cols)
    dma = pltpu.SemaphoreType.DMA
    any_spec = pl.BlockSpec(memory_space=pl.ANY)
    vm = pl.BlockSpec(memory_space=pltpu.VMEM)
    chunk_rows = 2 * toks // CHUNKS
    win, grad_att, up_all = pl.pallas_call(
        functools.partial(gather_kernel, planes, fsdp),
        out_shape=(
            jax.ShapeDtypeStruct((SPAN, 2, toks, width), BF16),
            jax.ShapeDtypeStruct((toks, width), BF16),
            jax.ShapeDtypeStruct((group, toks, cols), BF16),
        ),
        in_specs=[any_spec, vm, vm, any_spec],
        out_specs=(any_spec, vm, vm),
        scratch_shapes=[
            pltpu.VMEM((depth, width), BF16),
            pltpu.VMEM((fsdp, toks, depth), BF16),
            pltpu.VMEM((fsdp, toks, width), BF16),
            pltpu.VMEM((fsdp, toks, width), BF16),
            pltpu.VMEM((chunk_rows, width), BF16),
            dma((CHUNKS,)), dma((CHUNKS,)), dma((CHUNKS,)), dma((CHUNKS,)),
            dma((SPAN, CHUNKS)), dma((CHUNKS,)), dma,
            dma((fsdp,)), dma((fsdp,)), dma((fsdp,)), dma((fsdp,)),
            dma((SPAN, fsdp)), dma((SPAN, fsdp)), dma,
        ],
        compiler_params=pltpu.CompilerParams(collective_id=0, has_side_effects=True),
        name="gather",
    )(kv, up, up_cols, out_weight)

    lane = 2 * HEAD_DIM
    flat = pl.BlockSpec((toks, lane), lambda h: (0, h))
    pair = pl.BlockSpec((2, toks, lane), lambda h: (0, 0, h))
    wide = pl.BlockSpec((SPAN, 2, toks, lane), lambda h: (0, 0, 0, h))
    dq, att, dkv, dwin = pl.pallas_call(
        attend_kernel,
        grid=(width // lane,),
        out_shape=(
            jax.ShapeDtypeStruct((toks, width), BF16),
            jax.ShapeDtypeStruct((toks, width), BF16),
            jax.ShapeDtypeStruct((2, toks, width), F32),
            jax.ShapeDtypeStruct((SPAN, 2, toks, width), BF16),
        ),
        in_specs=[flat, pair, wide, flat],
        out_specs=(flat, flat, pair, wide),
        name="attend",
    )(queries[0], kv, win, grad_att)

    out_kv, out_w = pl.pallas_call(
        functools.partial(return_kernel_wrapped, planes, fsdp),
        out_shape=(
            jax.ShapeDtypeStruct((2, toks, width), BF16),
            jax.ShapeDtypeStruct((own_rows, width), F32),
        ),
        in_specs=[any_spec, any_spec, vm, vm],
        out_specs=(vm, vm),
        scratch_shapes=[
            pltpu.VMEM((2, toks, width), F32),
            dma,
            pltpu.VMEM((SPAN, 2, toks, width), BF16),
            pltpu.VMEM((2, toks, width), BF16),
            pltpu.VMEM((2, toks, width), BF16),
            pltpu.VMEM((2, toks, width), BF16),
            pltpu.VMEM((2, toks, width), BF16),
            pltpu.VMEM((group, toks, width), BF16),
            pltpu.VMEM((planes, own_rows, width), BF16),
            pltpu.VMEM((planes, own_rows, width), BF16),
            dma((SPAN,)),
            dma((CHUNKS,)), dma((CHUNKS,)), dma((CHUNKS,)), dma((CHUNKS,)),
            dma((CHUNKS,)), dma((CHUNKS,)), dma((CHUNKS,)), dma((CHUNKS,)),
            dma((2, fsdp)), dma((2, fsdp)), dma((2, fsdp)), dma((2, fsdp)),
            dma, dma((planes,)), dma((planes,)),
        ],
        compiler_params=pltpu.CompilerParams(collective_id=1, has_side_effects=True),
        name="give_back",
    )(dwin, dkv, att, up_all)
    return dq[None], jnp.swapaxes(out_kv, 0, 1)[None], out_w


def return_kernel_wrapped(planes, fsdp, dwin, dkv_hbm, att, up_all, out_kv, out_w, dkv, dkv_sem, *rest):
    copy = pltpu.make_async_copy(dkv_hbm, dkv, dkv_sem)
    copy.start()
    copy.wait()
    return_kernel(planes, fsdp, dwin, dkv, att, up_all, out_kv, out_w, *rest)


def solution(mesh):
    return jax.shard_map(
        shards,
        mesh=mesh,
        in_specs=(
            P("fsdp", "ctx", None),
            P("fsdp", "ctx", None, None),
            P("fsdp", "ctx", None),
            P("fsdp", None),
        ),
        out_specs=(P("fsdp", "ctx", None), P("fsdp", "ctx", None, None), P(("ctx", "fsdp"), None)),
        check_vma=False,
    )
```

```python
import functools

import jax
import jax.numpy as jnp
from jax import lax
from jax.experimental import pallas as pl
from jax.experimental.pallas import tpu as pltpu
from jax.sharding import PartitionSpec as P

HEADS = 16
HEAD_DIM = 128
SPAN = 4
WINDOW = 512
NEGATIVE = -1e30
CHUNKS = 8
AHEAD = 5
LAG = 2
F32 = jnp.float32
BF16 = jnp.bfloat16


class Place:
    def __init__(self, planes, fsdp):
        self.planes, self.fsdp = planes, fsdp
        me = lax.axis_index("ctx")
        self.f = lax.axis_index("fsdp")
        self.p = lax.div(me, SPAN)
        self.r = lax.rem(me, SPAN)
        self.core = lax.rem(self.r, 2)
        self.y = lax.div(self.r, 2)
        self.mate = self.r + 1 - 2 * self.core
        self.across = lax.rem(self.r + 2, SPAN)

    def dev(self, p, r, f):
        return {"ctx": p * SPAN + r, "fsdp": f}

    def members(self):
        for dr in range(SPAN):
            for df in range(self.fsdp):
                if dr or df:
                    yield lax.rem(self.r + dr, SPAN), lax.rem(self.f + df, self.fsdp), dr, df

    def barrier(self):
        sem = pltpu.get_barrier_semaphore()
        count = 0
        for r, f, _, _ in self.members():
            pl.semaphore_signal(sem, inc=1, device_id=self.dev(self.p, r, f), device_id_type=pl.DeviceIdType.MESH)
            count += 1
        for dp in range(1, self.planes):
            other = lax.rem(self.p + dp, self.planes)
            pl.semaphore_signal(sem, inc=1, device_id=self.dev(other, self.r, self.f), device_id_type=pl.DeviceIdType.MESH)
            count += 1
        pl.semaphore_wait(sem, count)


def remote(src, dst, send, recv, device):
    return pltpu.make_async_remote_copy(
        src_ref=src, dst_ref=dst, send_sem=send, recv_sem=recv, device_id=device, device_id_type=pl.DeviceIdType.MESH
    )


def chunk_cols(c, wide):
    return pl.ds(pl.multiple_of(c * wide, wide), wide)


def attend_head(q, ga, k, v, bias):
    inv_root = HEAD_DIM ** (-0.5)
    nt = (((1,), (1,)), ((), ()))
    tn = (((0,), (0,)), ((), ()))
    scores = lax.dot_general(q, k, nt, preferred_element_type=F32) * inv_root + bias
    lifted = jnp.exp(scores - jnp.max(scores, axis=-1, keepdims=True))
    prob = lifted * (1.0 / jnp.sum(lifted, axis=-1, keepdims=True))
    low = prob.astype(BF16)
    att = jnp.dot(low, v, preferred_element_type=F32).astype(BF16)
    products = lax.dot_general(ga, v, nt, preferred_element_type=F32)
    center = jnp.sum(ga.astype(F32) * att.astype(F32), axis=-1, keepdims=True)
    ds = (prob * (products - center)).astype(BF16)
    dq = (jnp.dot(ds, k, preferred_element_type=F32) * inv_root).astype(BF16)
    dk = lax.dot_general(ds, q, tn, preferred_element_type=F32) * inv_root
    dv = lax.dot_general(low, ga, tn, preferred_element_type=F32)
    return att, dq, dk, dv


def layer_kernel(
    planes, fsdp,
    q_ref, kv, up, up_cols, weight,
    dq_ref, out_kv, out_w,
    w_v, up_in, part_out, part_in, win, ga_ref, up_all, bias,
    g, dkv, share_in, y_in, c_in, z_in, att_all, w_out, w_in,
    fz_send, fy_send, fc_send, fs_send, slot_recv, w_sem, u_send, u_recv, q_send, q_recv, m_send, m_recv,
    sh_send, sh_recv, y_send, y_recv, c_send, c_recv, z_send, z_recv,
    a_send, a_recv, b_send, b_recv, r_send, r_recv,
):
    at = Place(planes, fsdp)
    toks = up.shape[0]
    depth = weight.shape[0]
    width = weight.shape[1]
    wide = width // CHUNKS
    f = at.f
    mine = at.r * fsdp + f
    mate_across = lax.rem(at.mate + 2, SPAN)
    mate = at.dev(at.p, at.mate, f)
    over = at.dev(at.p, at.across, f)
    w_copy = pltpu.make_async_copy(weight, w_v, w_sem)
    w_copy.start()

    @pl.when(at.p == 0)
    def _():
        win[at.r] = jnp.zeros(win.shape[1:], BF16)

    at.barrier()

    def cut(ref, c):
        return ref.at[:, :, chunk_cols(c, wide)]

    def up_copy(df):
        h = lax.rem(f + df, fsdp)
        return remote(
            up.at[:, pl.ds(pl.multiple_of(h * depth, 128), depth)], up_in.at[fsdp - df], u_send.at[df], u_recv.at[fsdp - df],
            at.dev(at.p, at.r, h),
        )

    def slot(j, c):
        return cut(win.at[j], c)

    def fz_copy(c):
        return remote(cut(kv, c), slot(at.r, c), fz_send.at[c], slot_recv.at[at.r, c], at.dev(at.p + 1, at.r, f))

    def fy_copy(c, src):
        return remote(src, slot(at.r, c), fy_send.at[c], slot_recv.at[at.r, c], over)

    def fc_copy(c, src):
        return remote(src, slot(at.r, c), fc_send.at[c], slot_recv.at[at.r, c], mate)

    def fs_copy(c):
        return remote(slot(at.across, c), slot(at.across, c), fs_send.at[c], slot_recv.at[at.across, c], mate)

    def arrived(j, c):
        remote(slot(j, c), slot(j, c), fz_send.at[c], slot_recv.at[j, c], mate).wait_recv()

    for df in range(1, fsdp):
        up_copy(df).start()

    def begin(c, _):
        @pl.when(at.p < planes - 1)
        def _():
            fz_copy(c).start()

        @pl.when(at.y == 0)
        def _():
            fy_copy(c, cut(kv, c)).start()

        @pl.when(at.core == 0)
        def _():
            fc_copy(c, cut(kv, c)).start()

        return 0

    lax.fori_loop(0, CHUNKS, begin, 0)

    row = lax.broadcasted_iota(jnp.int32, (toks, toks), 0)
    col = lax.broadcasted_iota(jnp.int32, (toks, toks), 1)
    for j in range(SPAN + 1):
        if j < SPAN:
            blocks = jnp.where(j < at.r, at.r - j, at.r - j + SPAN)
            limit = jnp.where(jnp.logical_and(at.p == 0, j >= at.r), 0, WINDOW)
        else:
            blocks, limit = 0, WINDOW
        distance = blocks * toks + row - col
        bias[:, j * toks : (j + 1) * toks] = jnp.where((distance >= 0) & (distance < limit), 0.0, NEGATIVE)

    w_copy.wait()
    tile = 512

    def product(lhs_of, put):
        def step(t, _):
            cols = chunk_cols(t, tile)
            put(cols, jnp.dot(lhs_of(), w_v[:, cols], preferred_element_type=F32))
            return 0

        lax.fori_loop(0, width // tile, step, 0)

    def part_copy(df):
        return remote(
            part_out.at[df], part_in.at[fsdp - df], q_send.at[df], q_recv.at[fsdp - df],
            at.dev(at.p, at.r, lax.rem(f + df, fsdp)),
        )

    for df in range(1, fsdp):
        remote(up_in.at[df], up_in.at[df], u_send.at[df], u_recv.at[df], at.dev(at.p, at.r, lax.rem(f + df, fsdp))).wait_recv()

        def put(cols, value, df=df):
            part_out[df, :, cols] = value.astype(BF16)

        product(lambda df=df: up_in[df], put)
        part_copy(df).start()

    def col_copy(r, h, dr, df):
        return remote(up_cols.at[r * fsdp + h], up_all.at[mine], m_send.at[dr, df], m_recv.at[dr, df], at.dev(at.p, r, h))

    for r, h, dr, df in at.members():
        col_copy(r, h, dr, df).start()
    up_all[mine] = up_cols[mine]

    def forward(c, _):
        @pl.when(at.p > 0)
        def _():
            arrived(at.r, c)

        @pl.when(at.y == 1)
        def _():
            fy_copy(c, slot(at.r, c)).start()

        @pl.when(at.core == 1)
        def _():
            fc_copy(c, slot(at.r, c)).start()

        arrived(at.across, c)
        fs_copy(c).start()
        return 0

    lax.fori_loop(0, AHEAD, forward, 0)
    own_depth = pl.ds(pl.multiple_of(f * depth, 128), depth)
    for df in range(1, fsdp):
        remote(part_in.at[df], part_in.at[df], q_send.at[df], q_recv.at[df], at.dev(at.p, at.r, lax.rem(f + df, fsdp))).wait_recv()

    def put_own(cols, value):
        for df in range(1, fsdp):
            value = value + part_in[df, :, cols].astype(F32)
        ga_ref[:, cols] = value.astype(BF16)

    product(lambda: up[:, own_depth], put_own)

    def peers():
        for half in range(2):
            for df in range(fsdp):
                yield half, df, lax.rem(at.r + 2 * half, SPAN), lax.rem(f + df, fsdp)

    def a_copy(half, df, r, h, view, c):
        return remote(view(att_all.at[mine]), view(att_all.at[mine]), a_send.at[half, df], a_recv.at[half, df, c], at.dev(at.p, r, h))

    def origin(half, df):
        return lax.rem(at.r + SPAN - 2 * half, SPAN) * fsdp + lax.rem(f + fsdp - df, fsdp)

    def b_copy(half, df, view, c):
        block = att_all.at[origin(half, df)]
        return remote(view(block), view(block), b_send.at[half, df], b_recv.at[half, df, c], mate)

    def whole(ref):
        return ref

    def sh_copy(c):
        return remote(cut(g.at[mate_across], c), cut(share_in, c), sh_send.at[c], sh_recv.at[c], mate)

    def c_copy(c):
        return remote(cut(g.at[at.mate], c), cut(c_in, c), c_send.at[c], c_recv.at[c], mate)

    def y_copy(c):
        return remote(cut(g.at[at.across], c), cut(y_in, c), y_send.at[c], y_recv.at[c], over)

    def z_copy(c):
        return remote(cut(g.at[at.r], c), cut(z_in, c), z_send.at[c], z_recv.at[c], at.dev(at.p - 1, at.r, f))

    def second(c, _):
        cols = chunk_cols(c, wide)
        sh_copy(c).wait_recv()
        g[at.across, :, :, cols] = (g[at.across, :, :, cols].astype(F32) + share_in[:, :, cols].astype(F32)).astype(BF16)
        y_copy(c).start()
        return 0

    def attend(c, _):
        @pl.when(c + AHEAD < CHUNKS)
        def _():
            forward(c + AHEAD, 0)

        arrived(at.mate, c)
        arrived(mate_across, c)
        for h in range(wide // HEAD_DIM):
            cols = pl.ds(pl.multiple_of(c * wide + h * HEAD_DIM, HEAD_DIM), HEAD_DIM)
            k = jnp.concatenate([win[j, 0, :, cols] for j in range(SPAN)] + [kv[0, :, cols]], axis=0)
            v = jnp.concatenate([win[j, 1, :, cols] for j in range(SPAN)] + [kv[1, :, cols]], axis=0)
            att, dq, dk, dv = attend_head(q_ref[:, cols], ga_ref[:, cols], k, v, bias[...])
            att_all[mine, :, cols] = att
            dq_ref[:, cols] = dq
            for j in range(SPAN):
                g[j, 0, :, cols] = dk[j * toks : (j + 1) * toks].astype(BF16)
                g[j, 1, :, cols] = dv[j * toks : (j + 1) * toks].astype(BF16)
            dkv[0, :, cols] = dk[SPAN * toks :]
            dkv[1, :, cols] = dv[SPAN * toks :]

        def view(ref):
            return ref.at[:, chunk_cols(c, wide)]

        for half, df, r, h in peers():
            if half or df:
                a_copy(half, df, r, h, view, c).start()
        b_copy(0, 0, view, c).start()
        sh_copy(c).start()
        c_copy(c).start()

        @pl.when(c >= LAG)
        def _():
            second(c - LAG, 0)

        return 0

    lax.fori_loop(0, CHUNKS, attend, 0)
    lax.fori_loop(CHUNKS - LAG, CHUNKS, second, 0)

    def third(c, _):
        cols = chunk_cols(c, wide)
        c_copy(c).wait_recv()
        y_copy(c).wait_recv()
        core_prev = at.core == 1
        y_prev = at.y == 1
        c_val = c_in[:, :, cols].astype(F32)
        y_val = y_in[:, :, cols].astype(F32)
        zero = jnp.zeros_like(c_val)
        prev = g[at.r, :, :, cols].astype(F32) + jnp.where(core_prev, c_val, zero) + jnp.where(y_prev, y_val, zero)
        g[at.r, :, :, cols] = prev.astype(BF16)
        dkv[:, :, cols] = dkv[:, :, cols] + jnp.where(core_prev, zero, c_val) + jnp.where(y_prev, zero, y_val)

        @pl.when(at.p > 0)
        def _():
            z_copy(c).start()

        return 0

    for r, h, dr, df in at.members():
        back = lax.rem(at.r + SPAN - dr, SPAN) * fsdp + lax.rem(f + fsdp - df, fsdp)
        remote(up_all.at[back], up_all.at[back], m_send.at[dr, df], m_recv.at[dr, df], at.dev(at.p, r, h)).wait_recv()
    own_rows = out_w.shape[0]
    tn = (((0,), (0,)), ((), ()))
    tokens = SPAN * fsdp * toks

    def r_copy(dp, view):
        other = lax.rem(at.p + dp, planes)
        return remote(
            view(w_out.at[other]), view(w_in.at[planes - dp]), r_send.at[dp], r_recv.at[planes - dp], at.dev(other, at.r, f)
        )

    def weigh(c, _):
        cols = chunk_cols(c, wide)

        def view(ref):
            return ref.at[:, cols]

        for half, df, r, h in peers():
            block = view(att_all.at[lax.rem(at.mate + SPAN - 2 * half, SPAN) * fsdp + lax.rem(f + fsdp - df, fsdp)])
            remote(block, block, b_send.at[half, df], b_recv.at[half, df, c], mate).wait_recv()
        lhs = up_all[...].reshape(tokens, up_all.shape[2])
        value = lax.dot_general(lhs, att_all[:, :, cols].reshape(tokens, wide), tn, preferred_element_type=F32)
        for n in range(planes):
            w_out[n, :, cols] = value[n * own_rows : (n + 1) * own_rows].astype(BF16)
        for dp in range(1, planes):
            r_copy(dp, view).start()
        return 0

    def relay(c, _):
        def view(ref):
            return ref.at[:, chunk_cols(c, wide)]

        for half, df, r, h in peers():
            if half or df:
                block = view(att_all.at[origin(half, df)])
                remote(block, block, a_send.at[half, df], a_recv.at[half, df, c], at.dev(at.p, r, h)).wait_recv()
                b_copy(half, df, view, c).start()

        @pl.when(c >= 1)
        def _():
            weigh(c - 1, 0)

        third(c, 0)
        return 0

    lax.fori_loop(0, CHUNKS, relay, 0)
    weigh(CHUNKS - 1, 0)

    def fourth(c, _):
        cols = chunk_cols(c, wide)

        @pl.when(at.p < planes - 1)
        def _():
            z_copy(c).wait_recv()
            out_kv[:, :, cols] = (dkv[:, :, cols] + z_in[:, :, cols].astype(F32)).astype(BF16)

        @pl.when(at.p == planes - 1)
        def _():
            out_kv[:, :, cols] = dkv[:, :, cols].astype(BF16)

        @pl.when(at.p < planes - 1)
        def _():
            fz_copy(c).wait_send()

        fy_copy(c, slot(at.r, c)).wait_send()
        fc_copy(c, slot(at.r, c)).wait_send()
        fs_copy(c).wait_send()
        sh_copy(c).wait_send()
        c_copy(c).wait_send()
        y_copy(c).wait_send()

        @pl.when(at.p > 0)
        def _():
            z_copy(c).wait_send()

        return 0

    lax.fori_loop(0, CHUNKS, fourth, 0)
    for df in range(1, fsdp):
        up_copy(df).wait_send()
        part_copy(df).wait_send()
    for r, h, dr, df in at.members():
        col_copy(r, h, dr, df).wait_send()
    for half, df, r, h in peers():
        if half or df:
            a_copy(half, df, r, h, whole, 0).wait_send()
        b_copy(half, df, whole, 0).wait_send()
    out_w[...] = w_out[at.p].astype(F32)
    for dp in range(1, planes):
        remote(w_in.at[dp], w_in.at[dp], r_send.at[dp], r_recv.at[dp], at.dev(lax.rem(at.p + dp, planes), at.r, f)).wait_recv()
        out_w[...] += w_in[dp].astype(F32)
    for dp in range(1, planes):
        r_copy(dp, whole).wait_send()


def shards(queries, keys_values, upstream, out_weight):
    seqs, toks, width = queries.shape
    ctx, fsdp = lax.axis_size("ctx"), lax.axis_size("fsdp")
    planes = ctx // SPAN
    model = upstream.shape[2]
    own_rows = model // (ctx * fsdp)
    group = SPAN * fsdp
    cols = planes * own_rows
    depth = out_weight.shape[0]
    kv = jnp.swapaxes(keys_values[0], 0, 1)
    up = upstream[0]
    up_cols = up.reshape(toks, planes, SPAN, fsdp, own_rows).transpose(2, 3, 0, 1, 4).reshape(group, toks, cols)
    dma = pltpu.SemaphoreType.DMA
    any_spec = pl.BlockSpec(memory_space=pl.ANY)
    vm = pl.BlockSpec(memory_space=pltpu.VMEM)
    block = (2, toks, width)
    line = dma((CHUNKS,))
    fan = dma((2, fsdp))
    spread = dma((2, fsdp, CHUNKS))
    dq, out_kv, out_w = pl.pallas_call(
        functools.partial(layer_kernel, planes, fsdp),
        out_shape=(
            jax.ShapeDtypeStruct((toks, width), BF16),
            jax.ShapeDtypeStruct(block, BF16),
            jax.ShapeDtypeStruct((own_rows, width), F32),
        ),
        in_specs=[vm, vm, vm, vm, any_spec],
        out_specs=(vm, vm, vm),
        scratch_shapes=[
            pltpu.VMEM((depth, width), BF16),
            pltpu.VMEM((fsdp, toks, depth), BF16),
            pltpu.VMEM((fsdp, toks, width), BF16),
            pltpu.VMEM((fsdp, toks, width), BF16),
            pltpu.VMEM((SPAN,) + block, BF16),
            pltpu.VMEM((toks, width), BF16),
            pltpu.VMEM((group, toks, cols), BF16),
            pltpu.VMEM((toks, (SPAN + 1) * toks), F32),
            pltpu.VMEM((SPAN,) + block, BF16),
            pltpu.VMEM(block, F32),
            pltpu.VMEM(block, BF16),
            pltpu.VMEM(block, BF16),
            pltpu.VMEM(block, BF16),
            pltpu.VMEM(block, BF16),
            pltpu.VMEM((group, toks, width), BF16),
            pltpu.VMEM((planes, own_rows, width), BF16),
            pltpu.VMEM((planes, own_rows, width), BF16),
            line, line, line, line, dma((SPAN, CHUNKS)), dma,
            dma((fsdp,)), dma((fsdp,)), dma((fsdp,)), dma((fsdp,)), dma((SPAN, fsdp)), dma((SPAN, fsdp)),
            line, line, line, line, line, line, line, line,
            fan, spread, fan, spread, dma((planes,)), dma((planes,)),
        ],
        compiler_params=pltpu.CompilerParams(collective_id=0, has_side_effects=True),
        name="layer",
    )(queries[0], kv, up, up_cols, out_weight)
    return dq[None], jnp.swapaxes(out_kv, 0, 1)[None], out_w


def solution(mesh):
    return jax.shard_map(
        shards,
        mesh=mesh,
        in_specs=(
            P("fsdp", "ctx", None),
            P("fsdp", "ctx", None, None),
            P("fsdp", "ctx", None),
            P("fsdp", None),
        ),
        out_specs=(P("fsdp", "ctx", None), P("fsdp", "ctx", None, None), P(("ctx", "fsdp"), None)),
        check_vma=False,
    )
```

```python
import functools

import jax
import jax.numpy as jnp
from jax import lax
from jax.experimental import pallas as pl
from jax.experimental.pallas import tpu as pltpu
from jax.sharding import PartitionSpec as P

HEADS = 16
HEAD_DIM = 128
SPAN = 4
WINDOW = 512
NEGATIVE = -1e30
CHUNKS = 8
AHEAD = 5
LAG = 2
DELAY = 4
F32 = jnp.float32
BF16 = jnp.bfloat16


class Place:
    def __init__(self, planes, fsdp):
        self.planes, self.fsdp = planes, fsdp
        me = lax.axis_index("ctx")
        self.f = lax.axis_index("fsdp")
        self.p = lax.div(me, SPAN)
        self.r = lax.rem(me, SPAN)
        self.core = lax.rem(self.r, 2)
        self.y = lax.div(self.r, 2)
        self.mate = self.r + 1 - 2 * self.core
        self.across = lax.rem(self.r + 2, SPAN)

    def dev(self, p, r, f):
        return {"ctx": p * SPAN + r, "fsdp": f}

    def members(self):
        for dr in range(SPAN):
            for df in range(self.fsdp):
                if dr or df:
                    yield lax.rem(self.r + dr, SPAN), lax.rem(self.f + df, self.fsdp), dr, df

    def barrier(self):
        sem = pltpu.get_barrier_semaphore()
        count = 0
        for r, f, _, _ in self.members():
            pl.semaphore_signal(sem, inc=1, device_id=self.dev(self.p, r, f), device_id_type=pl.DeviceIdType.MESH)
            count += 1
        for dp in range(1, self.planes):
            other = lax.rem(self.p + dp, self.planes)
            pl.semaphore_signal(sem, inc=1, device_id=self.dev(other, self.r, self.f), device_id_type=pl.DeviceIdType.MESH)
            count += 1
        pl.semaphore_wait(sem, count)


def remote(src, dst, send, recv, device):
    return pltpu.make_async_remote_copy(
        src_ref=src, dst_ref=dst, send_sem=send, recv_sem=recv, device_id=device, device_id_type=pl.DeviceIdType.MESH
    )


def chunk_cols(c, wide):
    return pl.ds(pl.multiple_of(c * wide, wide), wide)


def attend_head(q, ga, k, v, bias):
    inv_root = HEAD_DIM ** (-0.5)
    nt = (((1,), (1,)), ((), ()))
    tn = (((0,), (0,)), ((), ()))
    scores = lax.dot_general(q, k, nt, preferred_element_type=F32) * inv_root + bias
    lifted = jnp.exp(scores - jnp.max(scores, axis=-1, keepdims=True))
    prob = lifted * (1.0 / jnp.sum(lifted, axis=-1, keepdims=True))
    low = prob.astype(BF16)
    att = jnp.dot(low, v, preferred_element_type=F32).astype(BF16)
    products = lax.dot_general(ga, v, nt, preferred_element_type=F32)
    center = jnp.sum(ga.astype(F32) * att.astype(F32), axis=-1, keepdims=True)
    ds = (prob * (products - center)).astype(BF16)
    dq = (jnp.dot(ds, k, preferred_element_type=F32) * inv_root).astype(BF16)
    dk = lax.dot_general(ds, q, tn, preferred_element_type=F32) * inv_root
    dv = lax.dot_general(low, ga, tn, preferred_element_type=F32)
    return att, dq, dk, dv


def layer_kernel(
    planes, fsdp,
    q_ref, kv, up, up_cols, weight,
    dq_ref, out_kv, out_w,
    w_v, up_in, part_out, part_in, win, ga_ref, up_all, bias,
    g, dkv, share_in, y_in, c_in, z_in, att_all, w_out, w_in,
    fz_send, fy_send, fc_send, fs_send, slot_recv, w_sem, u_send, u_recv, q_send, q_recv, m_send, m_recv,
    sh_send, sh_recv, y_send, y_recv, c_send, c_recv, z_send, z_recv,
    a_send, a_recv, b_send, b_recv, r_send, r_recv,
):
    at = Place(planes, fsdp)
    toks = up.shape[0]
    depth = weight.shape[0]
    width = weight.shape[1]
    wide = width // CHUNKS
    f = at.f
    mine = at.r * fsdp + f
    mate_across = lax.rem(at.mate + 2, SPAN)
    mate = at.dev(at.p, at.mate, f)
    over = at.dev(at.p, at.across, f)
    w_copy = pltpu.make_async_copy(weight, w_v, w_sem)
    w_copy.start()

    @pl.when(at.p == 0)
    def _():
        win[at.r] = jnp.zeros(win.shape[1:], BF16)

    at.barrier()

    def cut(ref, c):
        return ref.at[:, :, chunk_cols(c, wide)]

    def up_copy(df):
        h = lax.rem(f + df, fsdp)
        return remote(
            up.at[:, pl.ds(pl.multiple_of(h * depth, 128), depth)], up_in.at[fsdp - df], u_send.at[df], u_recv.at[fsdp - df],
            at.dev(at.p, at.r, h),
        )

    def slot(j, c):
        return cut(win.at[j], c)

    def fz_copy(c):
        return remote(cut(kv, c), slot(at.r, c), fz_send.at[c], slot_recv.at[at.r, c], at.dev(at.p + 1, at.r, f))

    def fy_copy(c, src):
        return remote(src, slot(at.r, c), fy_send.at[c], slot_recv.at[at.r, c], over)

    def fc_copy(c, src):
        return remote(src, slot(at.r, c), fc_send.at[c], slot_recv.at[at.r, c], mate)

    def fs_copy(c):
        return remote(slot(at.across, c), slot(at.across, c), fs_send.at[c], slot_recv.at[at.across, c], mate)

    def arrived(j, c):
        remote(slot(j, c), slot(j, c), fz_send.at[c], slot_recv.at[j, c], mate).wait_recv()

    for df in range(1, fsdp):
        up_copy(df).start()

    def begin(c, _):
        @pl.when(at.p < planes - 1)
        def _():
            fz_copy(c).start()

        @pl.when(at.y == 0)
        def _():
            fy_copy(c, cut(kv, c)).start()

        @pl.when(at.core == 0)
        def _():
            fc_copy(c, cut(kv, c)).start()

        return 0

    lax.fori_loop(0, CHUNKS, begin, 0)

    row = lax.broadcasted_iota(jnp.int32, (toks, toks), 0)
    col = lax.broadcasted_iota(jnp.int32, (toks, toks), 1)
    for j in range(SPAN + 1):
        if j < SPAN:
            blocks = jnp.where(j < at.r, at.r - j, at.r - j + SPAN)
            limit = jnp.where(jnp.logical_and(at.p == 0, j >= at.r), 0, WINDOW)
        else:
            blocks, limit = 0, WINDOW
        distance = blocks * toks + row - col
        bias[:, j * toks : (j + 1) * toks] = jnp.where((distance >= 0) & (distance < limit), 0.0, NEGATIVE)

    w_copy.wait()
    tile = 512

    def product(lhs_of, put):
        def step(t, _):
            cols = chunk_cols(t, tile)
            put(cols, jnp.dot(lhs_of(), w_v[:, cols], preferred_element_type=F32))
            return 0

        lax.fori_loop(0, width // tile, step, 0)

    def part_copy(df):
        return remote(
            part_out.at[df], part_in.at[fsdp - df], q_send.at[df], q_recv.at[fsdp - df],
            at.dev(at.p, at.r, lax.rem(f + df, fsdp)),
        )

    for df in range(1, fsdp):
        remote(up_in.at[df], up_in.at[df], u_send.at[df], u_recv.at[df], at.dev(at.p, at.r, lax.rem(f + df, fsdp))).wait_recv()

        def put(cols, value, df=df):
            part_out[df, :, cols] = value.astype(BF16)

        product(lambda df=df: up_in[df], put)
        part_copy(df).start()

    def col_copy(r, h, dr, df):
        return remote(up_cols.at[r * fsdp + h], up_all.at[mine], m_send.at[dr, df], m_recv.at[dr, df], at.dev(at.p, r, h))

    for r, h, dr, df in at.members():
        col_copy(r, h, dr, df).start()
    up_all[mine] = up_cols[mine]

    def forward(c, _):
        @pl.when(at.p > 0)
        def _():
            arrived(at.r, c)

        @pl.when(at.y == 1)
        def _():
            fy_copy(c, slot(at.r, c)).start()

        @pl.when(at.core == 1)
        def _():
            fc_copy(c, slot(at.r, c)).start()

        arrived(at.across, c)
        fs_copy(c).start()
        return 0

    lax.fori_loop(0, AHEAD, forward, 0)
    own_depth = pl.ds(pl.multiple_of(f * depth, 128), depth)
    for df in range(1, fsdp):
        remote(part_in.at[df], part_in.at[df], q_send.at[df], q_recv.at[df], at.dev(at.p, at.r, lax.rem(f + df, fsdp))).wait_recv()

    def put_own(cols, value):
        for df in range(1, fsdp):
            value = value + part_in[df, :, cols].astype(F32)
        ga_ref[:, cols] = value.astype(BF16)

    product(lambda: up[:, own_depth], put_own)

    def peers():
        for half in range(2):
            for df in range(fsdp):
                yield half, df, lax.rem(at.r + 2 * half, SPAN), lax.rem(f + df, fsdp)

    def a_copy(half, df, r, h, view, c):
        return remote(view(att_all.at[mine]), view(att_all.at[mine]), a_send.at[half, df], a_recv.at[half, df, c], at.dev(at.p, r, h))

    def origin(half, df):
        return lax.rem(at.r + SPAN - 2 * half, SPAN) * fsdp + lax.rem(f + fsdp - df, fsdp)

    def b_copy(half, df, view, c):
        block = att_all.at[origin(half, df)]
        return remote(view(block), view(block), b_send.at[half, df], b_recv.at[half, df, c], mate)

    def whole(ref):
        return ref

    def sh_copy(c):
        return remote(cut(g.at[mate_across], c), cut(share_in, c), sh_send.at[c], sh_recv.at[c], mate)

    def c_copy(c):
        return remote(cut(g.at[at.mate], c), cut(c_in, c), c_send.at[c], c_recv.at[c], mate)

    def y_copy(c):
        return remote(cut(g.at[at.across], c), cut(y_in, c), y_send.at[c], y_recv.at[c], over)

    def z_copy(c):
        return remote(cut(g.at[at.r], c), cut(z_in, c), z_send.at[c], z_recv.at[c], at.dev(at.p - 1, at.r, f))

    def second(c, _):
        cols = chunk_cols(c, wide)
        sh_copy(c).wait_recv()
        g[at.across, :, :, cols] = (g[at.across, :, :, cols].astype(F32) + share_in[:, :, cols].astype(F32)).astype(BF16)
        y_copy(c).start()
        return 0

    def third(c, _):
        cols = chunk_cols(c, wide)
        c_copy(c).wait_recv()
        y_copy(c).wait_recv()
        core_prev = at.core == 1
        y_prev = at.y == 1
        c_val = c_in[:, :, cols].astype(F32)
        y_val = y_in[:, :, cols].astype(F32)
        zero = jnp.zeros_like(c_val)
        prev = g[at.r, :, :, cols].astype(F32) + jnp.where(core_prev, c_val, zero) + jnp.where(y_prev, y_val, zero)
        g[at.r, :, :, cols] = prev.astype(BF16)
        dkv[:, :, cols] = dkv[:, :, cols] + jnp.where(core_prev, zero, c_val) + jnp.where(y_prev, zero, y_val)

        @pl.when(at.p > 0)
        def _():
            z_copy(c).start()

        return 0

    for r, h, dr, df in at.members():
        back = lax.rem(at.r + SPAN - dr, SPAN) * fsdp + lax.rem(f + fsdp - df, fsdp)
        remote(up_all.at[back], up_all.at[back], m_send.at[dr, df], m_recv.at[dr, df], at.dev(at.p, r, h)).wait_recv()
    own_rows = out_w.shape[0]
    tn = (((0,), (0,)), ((), ()))
    tokens = SPAN * fsdp * toks

    def r_copy(dp, view):
        other = lax.rem(at.p + dp, planes)
        return remote(
            view(w_out.at[other]), view(w_in.at[planes - dp]), r_send.at[dp], r_recv.at[planes - dp], at.dev(other, at.r, f)
        )

    def weigh(c, _):
        cols = chunk_cols(c, wide)

        def view(ref):
            return ref.at[:, cols]

        for half, df, r, h in peers():
            block = view(att_all.at[lax.rem(at.mate + SPAN - 2 * half, SPAN) * fsdp + lax.rem(f + fsdp - df, fsdp)])
            remote(block, block, b_send.at[half, df], b_recv.at[half, df, c], mate).wait_recv()
        lhs = up_all[...].reshape(tokens, up_all.shape[2])
        value = lax.dot_general(lhs, att_all[:, :, cols].reshape(tokens, wide), tn, preferred_element_type=F32)
        for n in range(planes):
            w_out[n, :, cols] = value[n * own_rows : (n + 1) * own_rows].astype(BF16)
        for dp in range(1, planes):
            r_copy(dp, view).start()
        return 0

    def relay(c, _):
        def view(ref):
            return ref.at[:, chunk_cols(c, wide)]

        for half, df, r, h in peers():
            if half or df:
                block = view(att_all.at[origin(half, df)])
                remote(block, block, a_send.at[half, df], a_recv.at[half, df, c], at.dev(at.p, r, h)).wait_recv()
                b_copy(half, df, view, c).start()

        @pl.when(c >= 1)
        def _():
            weigh(c - 1, 0)

        third(c, 0)
        return 0

    def attend(c, _):
        @pl.when(c + AHEAD < CHUNKS)
        def _():
            forward(c + AHEAD, 0)

        arrived(at.mate, c)
        arrived(mate_across, c)
        for h in range(wide // HEAD_DIM):
            cols = pl.ds(pl.multiple_of(c * wide + h * HEAD_DIM, HEAD_DIM), HEAD_DIM)
            k = jnp.concatenate([win[j, 0, :, cols] for j in range(SPAN)] + [kv[0, :, cols]], axis=0)
            v = jnp.concatenate([win[j, 1, :, cols] for j in range(SPAN)] + [kv[1, :, cols]], axis=0)
            att, dq, dk, dv = attend_head(q_ref[:, cols], ga_ref[:, cols], k, v, bias[...])
            att_all[mine, :, cols] = att
            dq_ref[:, cols] = dq
            for j in range(SPAN):
                g[j, 0, :, cols] = dk[j * toks : (j + 1) * toks].astype(BF16)
                g[j, 1, :, cols] = dv[j * toks : (j + 1) * toks].astype(BF16)
            dkv[0, :, cols] = dk[SPAN * toks :]
            dkv[1, :, cols] = dv[SPAN * toks :]

        def view(ref):
            return ref.at[:, chunk_cols(c, wide)]

        for half, df, r, h in peers():
            if half or df:
                a_copy(half, df, r, h, view, c).start()
        b_copy(0, 0, view, c).start()
        sh_copy(c).start()
        c_copy(c).start()

        @pl.when(c >= LAG)
        def _():
            second(c - LAG, 0)

        @pl.when(c >= DELAY)
        def _():
            relay(c - DELAY, 0)

        return 0

    lax.fori_loop(0, CHUNKS, attend, 0)
    lax.fori_loop(CHUNKS - LAG, CHUNKS, second, 0)

    lax.fori_loop(CHUNKS - DELAY, CHUNKS, relay, 0)
    weigh(CHUNKS - 1, 0)

    def fourth(c, _):
        cols = chunk_cols(c, wide)

        @pl.when(at.p < planes - 1)
        def _():
            z_copy(c).wait_recv()
            out_kv[:, :, cols] = (dkv[:, :, cols] + z_in[:, :, cols].astype(F32)).astype(BF16)

        @pl.when(at.p == planes - 1)
        def _():
            out_kv[:, :, cols] = dkv[:, :, cols].astype(BF16)

        @pl.when(at.p < planes - 1)
        def _():
            fz_copy(c).wait_send()

        fy_copy(c, slot(at.r, c)).wait_send()
        fc_copy(c, slot(at.r, c)).wait_send()
        fs_copy(c).wait_send()
        sh_copy(c).wait_send()
        c_copy(c).wait_send()
        y_copy(c).wait_send()

        @pl.when(at.p > 0)
        def _():
            z_copy(c).wait_send()

        return 0

    lax.fori_loop(0, CHUNKS, fourth, 0)
    for df in range(1, fsdp):
        up_copy(df).wait_send()
        part_copy(df).wait_send()
    for r, h, dr, df in at.members():
        col_copy(r, h, dr, df).wait_send()
    for half, df, r, h in peers():
        if half or df:
            a_copy(half, df, r, h, whole, 0).wait_send()
        b_copy(half, df, whole, 0).wait_send()
    out_w[...] = w_out[at.p].astype(F32)
    for dp in range(1, planes):
        remote(w_in.at[dp], w_in.at[dp], r_send.at[dp], r_recv.at[dp], at.dev(lax.rem(at.p + dp, planes), at.r, f)).wait_recv()
        out_w[...] += w_in[dp].astype(F32)
    for dp in range(1, planes):
        r_copy(dp, whole).wait_send()


def shards(queries, keys_values, upstream, out_weight):
    seqs, toks, width = queries.shape
    ctx, fsdp = lax.axis_size("ctx"), lax.axis_size("fsdp")
    planes = ctx // SPAN
    model = upstream.shape[2]
    own_rows = model // (ctx * fsdp)
    group = SPAN * fsdp
    cols = planes * own_rows
    depth = out_weight.shape[0]
    kv = jnp.swapaxes(keys_values[0], 0, 1)
    up = upstream[0]
    up_cols = up.reshape(toks, planes, SPAN, fsdp, own_rows).transpose(2, 3, 0, 1, 4).reshape(group, toks, cols)
    dma = pltpu.SemaphoreType.DMA
    any_spec = pl.BlockSpec(memory_space=pl.ANY)
    vm = pl.BlockSpec(memory_space=pltpu.VMEM)
    block = (2, toks, width)
    line = dma((CHUNKS,))
    fan = dma((2, fsdp))
    spread = dma((2, fsdp, CHUNKS))
    dq, out_kv, out_w = pl.pallas_call(
        functools.partial(layer_kernel, planes, fsdp),
        out_shape=(
            jax.ShapeDtypeStruct((toks, width), BF16),
            jax.ShapeDtypeStruct(block, BF16),
            jax.ShapeDtypeStruct((own_rows, width), F32),
        ),
        in_specs=[vm, vm, vm, vm, any_spec],
        out_specs=(vm, vm, vm),
        scratch_shapes=[
            pltpu.VMEM((depth, width), BF16),
            pltpu.VMEM((fsdp, toks, depth), BF16),
            pltpu.VMEM((fsdp, toks, width), BF16),
            pltpu.VMEM((fsdp, toks, width), BF16),
            pltpu.VMEM((SPAN,) + block, BF16),
            pltpu.VMEM((toks, width), BF16),
            pltpu.VMEM((group, toks, cols), BF16),
            pltpu.VMEM((toks, (SPAN + 1) * toks), F32),
            pltpu.VMEM((SPAN,) + block, BF16),
            pltpu.VMEM(block, F32),
            pltpu.VMEM(block, BF16),
            pltpu.VMEM(block, BF16),
            pltpu.VMEM(block, BF16),
            pltpu.VMEM(block, BF16),
            pltpu.VMEM((group, toks, width), BF16),
            pltpu.VMEM((planes, own_rows, width), BF16),
            pltpu.VMEM((planes, own_rows, width), BF16),
            line, line, line, line, dma((SPAN, CHUNKS)), dma,
            dma((fsdp,)), dma((fsdp,)), dma((fsdp,)), dma((fsdp,)), dma((SPAN, fsdp)), dma((SPAN, fsdp)),
            line, line, line, line, line, line, line, line,
            fan, spread, fan, spread, dma((planes,)), dma((planes,)),
        ],
        compiler_params=pltpu.CompilerParams(collective_id=0, has_side_effects=True),
        name="layer",
    )(queries[0], kv, up, up_cols, out_weight)
    return dq[None], jnp.swapaxes(out_kv, 0, 1)[None], out_w


def solution(mesh):
    return jax.shard_map(
        shards,
        mesh=mesh,
        in_specs=(
            P("fsdp", "ctx", None),
            P("fsdp", "ctx", None, None),
            P("fsdp", "ctx", None),
            P("fsdp", None),
        ),
        out_specs=(P("fsdp", "ctx", None), P("fsdp", "ctx", None, None), P(("ctx", "fsdp"), None)),
        check_vma=False,
    )
```
